32 devices in a mesh: shot: 8 (over y, x, core), tm: 4 (over z).
Axes of the slice: x: 2, y: 2, z: 4, core: 2. Of those that a mesh axis runs over, the one named last changes fastest.
Arguments:
- records: bfloat16 [8, 16, 512], P('shot', None, 'tm'), may hold values from -6 to 6
- live: int32 [8, 16], P('shot'), may hold values 0 or 1
- dither: int32 [8], replicated, may hold values from 0 to 32, as said below
- designature: bfloat16 [9, 33], replicated, may hold values from -0.375 to 0.375
- first_weights: bfloat16 [64, 30], replicated, may hold values from -1.5 to 1.5
- first_bias: float32 [64], replicated, may hold values from -2.5 to 2.5
- hidden_weights: bfloat16 [3, 64, 192], replicated, may hold values from -0.625 to 0.625
- hidden_bias: float32 [3, 64], replicated, may hold values from -2.5 to 2.5
- out_weights: bfloat16 [64], replicated, may hold values from -0.75 to 0.75
- out_bias: float32 [1], replicated, may hold values from -2.5 to 2.5
- shaping: bfloat16 [9, 33], replicated, may hold values from -0.375 to 0.375
Outputs:
- interference: bfloat16 [8, 16, 512], P('shot', None, 'tm')
- cleaned: bfloat16 [8, 16, 512], P('shot', None, 'tm')
The draws below stay inside these ranges and needn't reach their ends.
Inputs may be any that keep to these rules, and one draw needn't show every extreme that they name: One shot's dither is exactly 32 and one shot's is 0.
All inputs are finite; a program needn't handle non-finite values. No bound on the sum of `live` on one device may be relied on, other than what follows from the above.
Results may differ from the reference program's by a relative error of at most 0.012.
The reference program's roundings to bfloat16 on the way count: a program that leaves them out, or rounds other values in their place, can miss the bound.
Values may be sent and summed in bfloat16 or wider, within the bound.
No kernel may reach another device: no remote copies, remote signals or barrier semaphores. Data moves between devices by JAX's collectives and lax.ppermute only.
A program may use at most 64 MiB of HBM per device.

```python
import jax
import jax.numpy as jnp
from jax import lax

CH = 64
HID = 3
FN = 9
FT = 33
SHOT_TAPS = 5
DMAX = 32
SHOTS = 8
NODES = 16
TIME = 512


def draw_dither(key, part):
    first_key, second_key = jax.random.split(jax.random.fold_in(key, 7))
    values = jax.random.randint(first_key, (SHOTS,), 0, DMAX + 1)
    spot = jax.random.randint(second_key, (), 0, SHOTS)
    values = values.at[spot].set(DMAX)
    values = values.at[(spot + 1) % SHOTS].set(0)
    return values.astype(jnp.int32)


def touch_ends(values, own_key, least, top_value):
    spot = [jax.random.randint(jax.random.fold_in(own_key, axis), (), 0, length) for axis, length in enumerate(values.shape)]
    main_axis = values.shape.index(max(values.shape))
    beside = spot[:main_axis] + [(spot[main_axis] + 1) % values.shape[main_axis]] + spot[main_axis + 1:]
    return values.at[tuple(spot)].set(least).at[tuple(beside)].set(top_value)


def level_of(stream_key, dims, shards, least, top_value):
    def one(position, blocks):
        draws = jax.random.uniform(jax.random.fold_in(jax.random.fold_in(stream_key, 6), position), (blocks,), jnp.float32, least / len(shards), top_value / len(shards))
        return jnp.repeat(jnp.exp(draws), dims[position] // blocks).reshape((-1,) + (1,) * (len(dims) - position - 1))

    factor_of = one(*shards[0])
    for cut in shards[1:]:
        factor_of = factor_of * one(*cut)
    return factor_of


def gaussian(key, extent, deviation, reach, pieces=(), held_as=jnp.bfloat16):
    values = jax.random.normal(key, extent, jnp.float32) * deviation
    if len(pieces) > 0:
        values = level_of(key, extent, pieces, -0.22, 0.18) * values
    return jnp.clip(values, min=-reach, max=reach).astype(held_as)


def setup_inputs(seed: int = 0) -> dict:
    key_list = jax.random.split(jax.random.key(seed), 12)
    return {
        "records": gaussian(key_list[0], (SHOTS, NODES, TIME), 1.0, 6.0, ((0, 8), (2, 4))),
        "live": touch_ends((jax.random.randint(key_list[1], (SHOTS, NODES), 0, 4) < 3).astype(jnp.int32), jax.random.fold_in(key_list[1], 1), 0, 1),
        "dither": draw_dither(jax.random.fold_in(key_list[11], 71), 0),
        "designature": gaussian(key_list[3], (FN, FT), (FN * FT) ** -0.5, 0.375),
        "first_weights": gaussian(key_list[4], (CH, 6 * SHOT_TAPS), (3 * SHOT_TAPS) ** -0.5, 1.5),
        "first_bias": gaussian(key_list[5], (CH,), 0.5, 2.5, (), jnp.float32),
        "hidden_weights": gaussian(key_list[6], (HID, CH, 3 * CH), (3 * CH // 2) ** -0.5, 0.625),
        "hidden_bias": gaussian(key_list[7], (HID, CH), 0.5, 2.5, (), jnp.float32),
        "out_weights": gaussian(key_list[8], (CH,), CH ** -0.5, 0.75),
        "out_bias": gaussian(key_list[9], (1,), 0.5, 2.5, (), jnp.float32),
        "shaping": gaussian(key_list[10], (FN, FT), (FN * FT) ** -0.5, 0.375),
    }


def shot_filter(traces, taps):
    result = lax.conv_general_dilated(
        traces.astype(jnp.float32)[:, None], taps.astype(jnp.float32)[None, None],
        (1, 1), ((FN // 2, FN // 2), (FT // 2, FT // 2)), precision=lax.Precision.HIGHEST)
    return result[:, 0]


def reference(records, live, dither, designature, first_weights, first_bias, hidden_weights, hidden_bias, out_weights, out_bias, shaping):
    keep = live[:, :, None] > 0
    masked = jnp.where(keep, records, jnp.zeros_like(records))
    filtered = jnp.where(keep, shot_filter(masked, designature), 0.0).astype(jnp.bfloat16)

    def one_gather(gather_rows):
        padded = jnp.pad(gather_rows, ((0, 0), (0, DMAX)))
        retimed = jax.vmap(lambda row, delay: lax.dynamic_slice_in_dim(row, delay, TIME))(padded, dither)
        inputs = jnp.stack([gather_rows, retimed]).astype(jnp.float32)
        shot_pad = jnp.pad(inputs, ((0, 0), (SHOT_TAPS // 2, SHOT_TAPS // 2), (1, 1)))
        columns = jnp.stack([shot_pad[channel, offset:offset + SHOTS, shift:shift + TIME]
                             for channel in range(2) for offset in range(SHOT_TAPS) for shift in range(3)])
        summed = jnp.einsum('of,fst->ost', first_weights.astype(jnp.float32), columns) + first_bias[:, None, None]
        active = jax.nn.relu(summed).astype(jnp.bfloat16)
        for layer in range(HID):
            dilation = 2 ** (layer + 1)
            padded_act = jnp.pad(active, ((0, 0), (0, 0), (dilation, dilation)))
            stacked = jnp.concatenate([padded_act[:, :, shift * dilation:shift * dilation + TIME] for shift in range(3)], axis=0)
            summed = jnp.einsum('of,fst->ost', hidden_weights[layer].astype(jnp.float32), stacked.astype(jnp.float32))
            summed = summed + hidden_bias[layer][:, None, None]
            active = jax.nn.relu(summed).astype(jnp.bfloat16)
        result = jnp.einsum('c,cst->st', out_weights.astype(jnp.float32), active.astype(jnp.float32)) + out_bias[0]
        return result.astype(jnp.bfloat16)

    predicted = lax.map(one_gather, jnp.transpose(filtered, (1, 0, 2)))
    predicted = jnp.transpose(predicted, (1, 0, 2))
    interference = jnp.where(keep, predicted, jnp.zeros_like(predicted))
    deblended = (filtered.astype(jnp.float32) - interference.astype(jnp.float32)).astype(jnp.bfloat16)
    cleaned = jnp.where(keep, shot_filter(deblended, shaping), 0.0).astype(jnp.bfloat16)
    return interference, cleaned
```

```python
import functools

import jax
import jax.numpy as jnp
from jax import lax
from jax.experimental import pallas as pl
from jax.experimental.pallas import tpu as pltpu
from jax.sharding import PartitionSpec as P

HID = 3
FN = 9
FT = 33
SHOT_TAPS = 5
DMAX = 32
LANES = 128
LEAD = 32
DEAD = 3e38
LIMIT = 1e38
F32 = jnp.float32
BF16 = jnp.bfloat16
AXES = ("shot", "tm")


def partners(shots, parts, rule):
    out = []
    for s in range(shots):
        for t in range(parts):
            a, b = rule(s, t)
            out.append((s * parts + t, a * parts + b))
    return out


def exchanges(shots, parts):
    def time_odd(s, t):
        o = ((t + 1) ^ 1) - 1
        return (s, o) if 0 <= o < parts else (s ^ 1, t)

    def pair_odd(s, t):
        o = ((s // 2 + 1) ^ 1) - 1
        return (2 * o + s % 2, t) if 0 <= o < shots // 2 else (s ^ 1, t)

    rules = (
        lambda s, t: (s, t ^ 1),
        time_odd,
        lambda s, t: (s ^ 1, t),
        lambda s, t: (s ^ 2, t),
        pair_odd,
    )
    return [partners(shots, parts, rule) for rule in rules]


def contract_lanes(a, b):
    return lax.dot_general(a, b, (((1,), (1,)), ((), ())), preferred_element_type=F32)


def prepare(info, designature, shaping, first_weights, biases, out_weights, tt1, tt2, w0, ow, bt, pad):
    window = tt1.shape[1]
    for taps, offset, out in ((designature, window - LANES - LEAD - FT // 2, tt1), (shaping, LEAD - FT // 2, tt2)):
        pad[...] = jnp.zeros_like(pad)
        pad[0:FN, 0:FT] = taps[...].astype(F32)
        for a in range(FN):
            row = jnp.broadcast_to(pad[a : a + 1, :], (LANES, window))
            row = pltpu.roll(row, offset, 1, stride=1, stride_axis=0)
            out[a * LANES : (a + 1) * LANES, :] = row.astype(BF16)
    parity = info[1] % 2
    columns = first_weights.shape[1]
    f = lax.broadcasted_iota(jnp.int32, (columns, w0.shape[1]), 0)
    g = lax.broadcasted_iota(jnp.int32, (columns, w0.shape[1]), 1)
    c, a, k = f // (3 * SHOT_TAPS), (f // 3) % SHOT_TAPS, f % 3
    here = (g // 16 == k) & ((g // 8) % 2 == c) & (g % 8 == a + parity)
    select = jnp.where(here, 1.0, 0.0).astype(BF16)
    w0[...] = jnp.dot(first_weights[...], select, preferred_element_type=F32).astype(BF16)
    channels = out_weights.shape[1]
    nodes = ow.shape[0]
    row = out_weights[...].astype(F32)
    row = jnp.concatenate([row] * (LANES // channels), axis=1)
    n = lax.broadcasted_iota(jnp.int32, (nodes, LANES), 0)
    for i in range(ow.shape[1] // LANES):
        m = (lax.broadcasted_iota(jnp.int32, (nodes, LANES), 1) + i * LANES) // channels
        ow[:, i * LANES : (i + 1) * LANES] = jnp.where(m == n, jnp.broadcast_to(row, n.shape), 0.0).astype(BF16)
    pad[...] = jnp.zeros_like(pad)
    pad[0 : biases.shape[0], 0:channels] = biases[...]
    bt[...] = jnp.transpose(pad[0:8, 0:LANES])


def deblend(
    total,
    shots,
    info,
    dither,
    out_bias,
    pair,
    first,
    second,
    tt1,
    tt2,
    w0,
    hidden,
    bt,
    ow,
    interference,
    cleaned,
    xs,
    yp,
    gs,
    zp,
):
    nodes, samples = interference.shape
    windows = samples // LANES + 1
    span = windows * LANES
    window = 2 * LANES
    channels = w0.shape[0]
    t, s = info[0], info[1]
    chip = s // 2
    even = chip % 2 == 0
    lowest, highest = chip == 0, chip == shots // 2 - 1
    stride = nodes + 8
    live = []
    for j in range(6):
        if 2 <= j < 4:
            x = pair[j - 2].astype(F32)
        else:
            p, q = (second, first) if j < 2 else (first, second)
            x = jnp.where(even, p[j % 2].astype(F32), q[j % 2].astype(F32))
            x = jnp.where(lowest if j < 2 else highest, 0.0, x)
        live.append(x[:, LANES : LANES + 1] < LIMIT)
        x = jnp.where(x < LIMIT, x, 0.0).astype(BF16)
        for w in range(windows):
            row = (w * 6 + j) * nodes
            xs[row : row + nodes, :] = x[:, w * LANES : w * LANES + window]
    blocks = windows * 6
    yp[...] = jnp.zeros_like(yp)
    y = contract_lanes(xs[...], tt1[...])
    for q in range(blocks):
        yp[8 + q * stride : 8 + q * stride + nodes, :] = y[q * nodes : (q + 1) * nodes, :]
    position = t * samples - LEAD + lax.broadcasted_iota(jnp.int32, (1, span), 1)
    valid = (position >= 0) & (position < total)
    gs[...] = jnp.zeros_like(gs)
    filtered = []
    for j in range(6):
        tiles = []
        for w in range(windows):
            base = 8 + (w * 6 + j) * stride - FN // 2
            acc = None
            for a in range(FN):
                v = yp[base + a : base + a + nodes, a * LANES : (a + 1) * LANES]
                acc = v if acc is None else acc + v
            tiles.append(acc)
        f = jnp.concatenate(tiles, axis=1)
        f = jnp.where(live[j] & valid, f, 0.0).astype(BF16).astype(F32)
        filtered.append(f)
        shot = jnp.clip(2 * chip - 2 + j, 0, shots - 1)
        r = pltpu.roll(f, span - dither[shot], 1)
        r = jnp.where(valid, r, 0.0)
        for w in range(windows):
            row = w * nodes * 16 + j
            gs[pl.ds(row, nodes, stride=16), :] = f[:, w * LANES : (w + 1) * LANES]
            gs[pl.ds(row + 8, nodes, stride=16), :] = r[:, w * LANES : (w + 1) * LANES]
    g = jnp.concatenate([gs[w * nodes * 16 : (w + 1) * nodes * 16, :] for w in range(windows)], axis=1)
    shifted = [pltpu.roll(g, 1, 1).astype(BF16), g.astype(BF16), pltpu.roll(g, span - 1, 1).astype(BF16)]
    acts = []
    for n in range(nodes):
        columns = jnp.concatenate([v[16 * n : 16 * n + 16, :] for v in shifted], axis=0)
        act = jnp.dot(w0[...], columns, preferred_element_type=F32) + bt[0:channels, 0:1]
        act = jnp.where(valid, jnp.maximum(act, 0.0), 0.0)
        for layer in range(HID):
            e = 2 ** (layer + 1)
            columns = jnp.concatenate(
                [pltpu.roll(act, e, 1).astype(BF16), act.astype(BF16), pltpu.roll(act, span - e, 1).astype(BF16)],
                axis=0,
            )
            act = jnp.dot(hidden[layer], columns, preferred_element_type=F32)
            act = act + bt[0:channels, layer + 1 : layer + 2]
            act = jnp.where(valid, jnp.maximum(act, 0.0), 0.0)
        acts.append(act.astype(BF16))
    pred = jnp.dot(ow[...], jnp.concatenate(acts, axis=0), preferred_element_type=F32) + out_bias[0]
    pred = pred.astype(BF16).astype(F32)
    odd = s % 2 == 1
    own = jnp.where(odd, filtered[3], filtered[2])
    alive = jnp.where(odd, live[3].astype(F32), live[2].astype(F32)) > 0.5
    pred = jnp.where(alive & valid, pred, 0.0)
    interference[...] = pltpu.roll(pred, span - LEAD, 1)[:, 0:samples].astype(BF16)
    difference = (own - pred).astype(BF16)
    zp[...] = jnp.zeros_like(zp)
    for w in range(samples // LANES):
        zp[8 : 8 + nodes, :] = contract_lanes(difference[:, w * LANES : w * LANES + window], tt2[...])
        acc = None
        for a in range(FN):
            v = zp[8 + a - FN // 2 : 8 + a - FN // 2 + nodes, a * LANES : (a + 1) * LANES]
            acc = v if acc is None else acc + v
        cleaned[:, w * LANES : (w + 1) * LANES] = jnp.where(alive, acc, 0.0).astype(BF16)


def local(
    records,
    live,
    dither,
    designature,
    first_weights,
    first_bias,
    hidden_weights,
    hidden_bias,
    out_weights,
    out_bias,
    shaping,
    shots,
    parts,
):
    _, nodes, samples = records.shape
    channels = first_weights.shape[0]
    total = samples * parts
    window = 2 * LANES
    windows = samples // LANES + 1
    span = windows * LANES
    s, t = lax.axis_index("shot"), lax.axis_index("tm")
    time_even, time_odd, partner, pair_even, pair_odd = exchanges(shots, parts)
    send = lambda x, pairs: lax.ppermute(x, AXES, pairs)

    info = jnp.stack([t, s]).astype(jnp.int32)
    vmem = pl.BlockSpec(memory_space=pltpu.VMEM)
    smem = pl.BlockSpec(memory_space=pltpu.SMEM)
    biases = jnp.concatenate([first_bias[None], hidden_bias], axis=0)
    tt1, tt2, w0, ow, bt = pl.pallas_call(
        prepare,
        out_shape=(
            jax.ShapeDtypeStruct((FN * LANES, window), BF16),
            jax.ShapeDtypeStruct((FN * LANES, window), BF16),
            jax.ShapeDtypeStruct((channels, 48), BF16),
            jax.ShapeDtypeStruct((nodes, nodes * channels), BF16),
            jax.ShapeDtypeStruct((LANES, 8), F32),
        ),
        in_specs=[smem] + [vmem] * 5,
        out_specs=(vmem,) * 5,
        scratch_shapes=[pltpu.VMEM((16, window), F32)],
        name="prepare",
    )(info, designature, shaping, first_weights, biases, out_weights[None])

    x = jnp.where(live[:, :, None] > 0, records, jnp.asarray(DEAD, BF16))
    a, b = send(x, time_even), send(x, time_odd)
    t_even = t % 2 == 0
    none = jnp.zeros_like(x)
    left = jnp.where(t == 0, none, jnp.where(t_even, b, a))
    right = jnp.where(t == parts - 1, none, jnp.where(t_even, a, b))
    x = jnp.concatenate([left, x, right], axis=2)
    y = send(x, partner)
    s_even = s % 2 == 0
    pair = jnp.concatenate([jnp.where(s_even, x, y), jnp.where(s_even, y, x)], axis=0)
    first, second = send(pair, pair_even), send(pair, pair_odd)

    rows = windows * 6 * nodes
    interference, cleaned = pl.pallas_call(
        functools.partial(deblend, total, shots),
        out_shape=(jax.ShapeDtypeStruct((nodes, samples), BF16),) * 2,
        in_specs=[smem] * 3 + [vmem] * 9,
        out_specs=(vmem,) * 2,
        scratch_shapes=[
            pltpu.VMEM((rows, window), BF16),
            pltpu.VMEM((windows * 6 * (nodes + 8) + 8, FN * LANES), F32),
            pltpu.VMEM((windows * nodes * 16, LANES), F32),
            pltpu.VMEM((nodes + 16, FN * LANES), F32),
        ],
        name="deblend",
    )(info, dither, out_bias, pair, first, second, tt1, tt2, w0, hidden_weights, bt, ow)
    return interference[None], cleaned[None]


def solution(mesh):
    shots, parts = mesh.shape["shot"], mesh.shape["tm"]
    in_specs = (P("shot", None, "tm"), P("shot", None), P(), P(), P(), P(), P(), P(), P(), P(), P())
    out_specs = (P("shot", None, "tm"), P("shot", None, "tm"))
    body = functools.partial(local, shots=shots, parts=parts)
    return jax.shard_map(body, mesh=mesh, in_specs=in_specs, out_specs=out_specs, check_vma=False)
```

```python
import functools

import jax
import jax.numpy as jnp
from jax import lax
from jax.experimental import pallas as pl
from jax.experimental.pallas import tpu as pltpu
from jax.sharding import PartitionSpec as P

HID = 3
FN = 9
FT = 33
SHOT_TAPS = 5
DMAX = 32
LANES = 128
VMEM_LIMIT = 24 * 2**20
LEAD = 32
DEAD = 3e38
LIMIT = 1e38
F32 = jnp.float32
BF16 = jnp.bfloat16
AXES = ("shot", "tm")


def partners(shots, parts, rule):
    out = []
    for s in range(shots):
        for t in range(parts):
            a, b = rule(s, t)
            out.append((s * parts + t, a * parts + b))
    return out


def exchanges(shots, parts):
    def time_odd(s, t):
        o = ((t + 1) ^ 1) - 1
        return (s, o) if 0 <= o < parts else (s ^ 1, t)

    def pair_odd(s, t):
        o = ((s // 2 + 1) ^ 1) - 1
        return (2 * o + s % 2, t) if 0 <= o < shots // 2 else (s ^ 1, t)

    rules = (
        lambda s, t: (s, t ^ 1),
        time_odd,
        lambda s, t: (s ^ 1, t),
        lambda s, t: (s ^ 2, t),
        pair_odd,
    )
    return [partners(shots, parts, rule) for rule in rules]


def contract_lanes(a, b):
    return lax.dot_general(a, b, (((1,), (1,)), ((), ())), preferred_element_type=F32)


def prepare(designature, shaping, first_weights, first_bias, hidden_bias, out_weights, tt1, tt2, w0, ow, bt, pad):
    window = tt1.shape[1]
    for taps, offset, out in ((designature, window - LANES - LEAD - FT // 2, tt1), (shaping, LEAD - FT // 2, tt2)):
        pad[...] = jnp.zeros_like(pad)
        pad[0:FN, 0:FT] = taps[...].astype(F32)
        for a in range(FN):
            row = jnp.broadcast_to(pad[a : a + 1, :], (LANES, window))
            row = pltpu.roll(row, offset, 1, stride=1, stride_axis=0)
            out[a * LANES : (a + 1) * LANES, :] = row.astype(BF16)
    parity = lax.axis_index("shot") % 2
    columns = first_weights.shape[0]
    f = lax.broadcasted_iota(jnp.int32, (columns, w0.shape[1]), 0)
    g = lax.broadcasted_iota(jnp.int32, (columns, w0.shape[1]), 1)
    c, a, k = f // (3 * SHOT_TAPS), (f // 3) % SHOT_TAPS, f % 3
    here = (g // 16 == k) & ((g // 8) % 2 == c) & (g % 8 == a + parity)
    select = jnp.where(here, 1.0, 0.0).astype(BF16)
    w0[...] = lax.dot_general(
        first_weights[...], select, (((0,), (0,)), ((), ())), preferred_element_type=F32
    ).astype(BF16)
    channels = out_weights.shape[1]
    nodes = ow.shape[0]
    row = out_weights[...].astype(F32)
    row = jnp.concatenate([row] * (LANES // channels), axis=1)
    n = lax.broadcasted_iota(jnp.int32, (nodes, LANES), 0)
    for i in range(ow.shape[1] // LANES):
        m = (lax.broadcasted_iota(jnp.int32, (nodes, LANES), 1) + i * LANES) // channels
        ow[:, i * LANES : (i + 1) * LANES] = jnp.where(m == n, jnp.broadcast_to(row, n.shape), 0.0).astype(BF16)
    pad[...] = jnp.zeros_like(pad)
    pad[0:1, 0:channels] = first_bias[...]
    pad[1 : HID + 1, 0:channels] = hidden_bias[...]
    bt[...] = jnp.transpose(pad[0:8, 0:LANES])


def deblend(
    total,
    shots,
    dither,
    out_bias,
    pair,
    first,
    second,
    tt1,
    tt2,
    w0,
    hidden,
    bt,
    ow,
    interference,
    cleaned,
    xs,
    yp,
    gs,
    zp,
):
    nodes, samples = interference.shape
    windows = samples // LANES + 1
    span = windows * LANES
    window = 2 * LANES
    channels = w0.shape[0]
    t, s = lax.axis_index("tm"), lax.axis_index("shot")
    chip = s // 2
    even = chip % 2 == 0
    lowest, highest = chip == 0, chip == shots // 2 - 1
    stride = nodes + 8
    live = []
    for j in range(6):
        if 2 <= j < 4:
            x = pair[j - 2].astype(F32)
        else:
            p, q = (second, first) if j < 2 else (first, second)
            x = jnp.where(even, p[j % 2].astype(F32), q[j % 2].astype(F32))
            x = jnp.where(lowest if j < 2 else highest, 0.0, x)
        live.append(x[:, LANES : LANES + 1] < LIMIT)
        x = jnp.where(x < LIMIT, x, 0.0).astype(BF16)
        for w in range(windows):
            row = (w * 6 + j) * nodes
            xs[row : row + nodes, :] = x[:, w * LANES : w * LANES + window]
    blocks = windows * 6
    yp[...] = jnp.zeros_like(yp)
    y = contract_lanes(xs[...], tt1[...])
    for q in range(blocks):
        yp[8 + q * stride : 8 + q * stride + nodes, :] = y[q * nodes : (q + 1) * nodes, :]
    position = t * samples - LEAD + lax.broadcasted_iota(jnp.int32, (1, span), 1)
    valid = (position >= 0) & (position < total)
    gs[...] = jnp.zeros_like(gs)
    filtered = []
    for j in range(6):
        tiles = []
        for w in range(windows):
            base = 8 + (w * 6 + j) * stride - FN // 2
            acc = None
            for a in range(FN):
                v = yp[base + a : base + a + nodes, a * LANES : (a + 1) * LANES]
                acc = v if acc is None else acc + v
            tiles.append(acc)
        f = jnp.concatenate(tiles, axis=1)
        f = jnp.where(live[j] & valid, f, 0.0).astype(BF16).astype(F32)
        filtered.append(f)
        shot = jnp.clip(2 * chip - 2 + j, 0, shots - 1)
        r = pltpu.roll(f, span - dither[shot], 1)
        r = jnp.where(valid, r, 0.0)
        for w in range(windows):
            row = w * nodes * 16 + j
            gs[pl.ds(row, nodes, stride=16), :] = f[:, w * LANES : (w + 1) * LANES]
            gs[pl.ds(row + 8, nodes, stride=16), :] = r[:, w * LANES : (w + 1) * LANES]
    g = jnp.concatenate([gs[w * nodes * 16 : (w + 1) * nodes * 16, :] for w in range(windows)], axis=1)
    shifted = [pltpu.roll(g, 1, 1).astype(BF16), g.astype(BF16), pltpu.roll(g, span - 1, 1).astype(BF16)]
    acts = []
    for n in range(nodes):
        columns = jnp.concatenate([v[16 * n : 16 * n + 16, :] for v in shifted], axis=0)
        act = jnp.dot(w0[...], columns, preferred_element_type=F32) + bt[0:channels, 0:1]
        acts.append(jnp.where(valid, jnp.maximum(act, 0.0), 0.0))
    for layer in range(HID):
        e = 2 ** (layer + 1)
        bias = bt[0:channels, layer + 1 : layer + 2]
        for n in range(nodes):
            act = acts[n]
            columns = jnp.concatenate(
                [pltpu.roll(act, e, 1).astype(BF16), act.astype(BF16), pltpu.roll(act, span - e, 1).astype(BF16)],
                axis=0,
            )
            act = jnp.dot(hidden[layer], columns, preferred_element_type=F32) + bias
            acts[n] = jnp.where(valid, jnp.maximum(act, 0.0), 0.0)
    acts = [act.astype(BF16) for act in acts]
    pred = jnp.dot(ow[...], jnp.concatenate(acts, axis=0), preferred_element_type=F32) + out_bias[0]
    pred = pred.astype(BF16).astype(F32)
    odd = s % 2 == 1
    own = jnp.where(odd, filtered[3], filtered[2])
    alive = jnp.where(odd, live[3].astype(F32), live[2].astype(F32)) > 0.5
    pred = jnp.where(alive & valid, pred, 0.0)
    interference[...] = pltpu.roll(pred, span - LEAD, 1)[:, 0:samples].astype(BF16)
    difference = (own - pred).astype(BF16)
    zp[...] = jnp.zeros_like(zp)
    for w in range(samples // LANES):
        zp[8 : 8 + nodes, :] = contract_lanes(difference[:, w * LANES : w * LANES + window], tt2[...])
        acc = None
        for a in range(FN):
            v = zp[8 + a - FN // 2 : 8 + a - FN // 2 + nodes, a * LANES : (a + 1) * LANES]
            acc = v if acc is None else acc + v
        cleaned[:, w * LANES : (w + 1) * LANES] = jnp.where(alive, acc, 0.0).astype(BF16)


def local(
    records,
    live,
    dither,
    designature,
    first_weights,
    first_bias,
    hidden_weights,
    hidden_bias,
    out_weights,
    out_bias,
    shaping,
    shots,
    parts,
):
    _, nodes, samples = records.shape
    channels = first_weights.shape[0]
    total = samples * parts
    window = 2 * LANES
    windows = samples // LANES + 1
    span = windows * LANES
    s, t = lax.axis_index("shot"), lax.axis_index("tm")
    time_even, time_odd, partner, pair_even, pair_odd = exchanges(shots, parts)
    send = lambda x, pairs: lax.ppermute(x, AXES, pairs)

    vmem = pl.BlockSpec(memory_space=pltpu.VMEM)
    smem = pl.BlockSpec(memory_space=pltpu.SMEM)
    tt1, tt2, w0, ow, bt = pl.pallas_call(
        prepare,
        out_shape=(
            jax.ShapeDtypeStruct((FN * LANES, window), BF16),
            jax.ShapeDtypeStruct((FN * LANES, window), BF16),
            jax.ShapeDtypeStruct((channels, 48), BF16),
            jax.ShapeDtypeStruct((nodes, nodes * channels), BF16),
            jax.ShapeDtypeStruct((LANES, 8), F32),
        ),
        in_specs=[vmem] * 6,
        out_specs=(vmem,) * 5,
        scratch_shapes=[pltpu.VMEM((16, window), F32)],
        compiler_params=pltpu.CompilerParams(vmem_limit_bytes=VMEM_LIMIT),
        cost_estimate=pl.CostEstimate(flops=4 * 10**6, bytes_accessed=10**6, transcendentals=0),
        name="prepare",
    )(designature, shaping, first_weights.T, first_bias[None], hidden_bias, out_weights[None])

    x = records
    a, b = send(x, time_even), send(x, time_odd)
    t_even = t % 2 == 0
    none = jnp.zeros_like(x)
    left = jnp.where(t == 0, none, jnp.where(t_even, b, a))
    right = jnp.where(t == parts - 1, none, jnp.where(t_even, a, b))
    x = jnp.concatenate([left, x, right], axis=2)
    x = jnp.where(live[:, :, None] > 0, x, jnp.asarray(DEAD, BF16))
    y = send(x, partner)
    s_even = s % 2 == 0
    pair = jnp.concatenate([jnp.where(s_even, x, y), jnp.where(s_even, y, x)], axis=0)
    first, second = send(pair, pair_even), send(pair, pair_odd)

    rows = windows * 6 * nodes
    interference, cleaned = pl.pallas_call(
        functools.partial(deblend, total, shots),
        out_shape=(jax.ShapeDtypeStruct((nodes, samples), BF16),) * 2,
        in_specs=[smem] * 2 + [vmem] * 9,
        out_specs=(vmem,) * 2,
        scratch_shapes=[
            pltpu.VMEM((rows, window), BF16),
            pltpu.VMEM((windows * 6 * (nodes + 8) + 8, FN * LANES), F32),
            pltpu.VMEM((windows * nodes * 16, LANES), F32),
            pltpu.VMEM((nodes + 16, FN * LANES), F32),
        ],
        compiler_params=pltpu.CompilerParams(vmem_limit_bytes=VMEM_LIMIT),
        cost_estimate=pl.CostEstimate(flops=4 * 10**8, bytes_accessed=10**6, transcendentals=0),
        name="deblend",
    )(dither, out_bias, pair, first, second, tt1, tt2, w0, hidden_weights, bt, ow)
    return interference[None], cleaned[None]


def solution(mesh):
    shots, parts = mesh.shape["shot"], mesh.shape["tm"]
    in_specs = (P("shot", None, "tm"), P("shot", None), P(), P(), P(), P(), P(), P(), P(), P(), P())
    out_specs = (P("shot", None, "tm"), P("shot", None, "tm"))
    body = functools.partial(local, shots=shots, parts=parts)
    return jax.shard_map(body, mesh=mesh, in_specs=in_specs, out_specs=out_specs, check_vma=False)
```

```python
import functools

import jax
import jax.numpy as jnp
from jax import lax
from jax.experimental import pallas as pl
from jax.experimental.pallas import tpu as pltpu
from jax.sharding import PartitionSpec as P

HID = 3
FN = 9
FT = 33
SHOT_TAPS = 5
DMAX = 32
LANES = 128
VMEM_LIMIT = 24 * 2**20
LEAD = 32
BEFORE = LEAD + FT // 2
DEAD = 3e38
LIMIT = 1e38
OFF = 1e30
F32 = jnp.float32
BF16 = jnp.bfloat16
AXES = ("shot", "tm")


def partners(shots, parts, rule):
    out = []
    for s in range(shots):
        for t in range(parts):
            a, b = rule(s, t)
            out.append((s * parts + t, a * parts + b))
    return out


def exchanges(shots, parts):
    def time_odd(s, t):
        o = ((t + 1) ^ 1) - 1
        return (s, o) if 0 <= o < parts else (s ^ 1, t)

    def pair_odd(s, t):
        o = ((s // 2 + 1) ^ 1) - 1
        return (2 * o + s % 2, t) if 0 <= o < shots // 2 else (s ^ 1, t)

    rules = (
        lambda s, t: (s, t ^ 1),
        time_odd,
        lambda s, t: (s ^ 1, t),
        lambda s, t: (s ^ 2, t),
        pair_odd,
    )
    return [partners(shots, parts, rule) for rule in rules]


def contract_lanes(a, b):
    return lax.dot_general(a, b, (((1,), (1,)), ((), ())), preferred_element_type=F32)


def extras(column, lanes, start):
    high = column.astype(BF16).astype(F32)
    middle = (column - high).astype(BF16).astype(F32)
    low = column - high - middle
    out = jnp.where(lanes == start, high, 0.0)
    out = jnp.where(lanes == start + 1, middle, out)
    out = jnp.where(lanes == start + 2, low, out)
    return jnp.where(lanes == start + 3, -OFF, out)


def prepare(
    dither, designature, shaping, first_weights, first_bias, hidden_weights, hidden_bias, out_weights, out_bias,
    tt1, tt2, w0, wh, ow, small, pad
):
    window = tt1.shape[1]
    for taps, offset, out in ((designature, 0, tt1), (shaping, LEAD - FT // 2, tt2)):
        pad[...] = jnp.zeros_like(pad)
        pad[0:FN, 0:FT] = taps[...].astype(F32)
        for a in range(FN):
            row = jnp.broadcast_to(pad[a : a + 1, :], (LANES, window))
            row = pltpu.roll(row, offset, 1, stride=1, stride_axis=0)
            out[a * LANES : (a + 1) * LANES, :] = row.astype(BF16)
    channels = out_weights.shape[1]
    pad[...] = jnp.zeros_like(pad)
    pad[0:1, 0:channels] = first_bias[...]
    pad[1 : HID + 1, 0:channels] = hidden_bias[...]
    bias = jnp.transpose(pad[0:8, 0:LANES])[0:channels, :]
    parity = lax.axis_index("shot") % 2
    columns = first_weights.shape[0]
    f = lax.broadcasted_iota(jnp.int32, (columns, w0.shape[1]), 0)
    g = lax.broadcasted_iota(jnp.int32, (columns, w0.shape[1]), 1)
    c, a, k = f // (3 * SHOT_TAPS), (f // 3) % SHOT_TAPS, f % 3
    here = (g // 16 == k) & ((g // 8) % 2 == c) & (g % 8 == a + parity)
    select = jnp.where(here, 1.0, 0.0).astype(BF16)
    value = lax.dot_general(first_weights[...], select, (((0,), (0,)), ((), ())), preferred_element_type=F32)
    lanes = lax.broadcasted_iota(jnp.int32, w0.shape, 1)
    w0[...] = (value + extras(bias[:, 0:1], lanes, 48)).astype(BF16)
    taps = hidden_weights.shape[2]
    unit = jnp.where(
        lax.broadcasted_iota(jnp.int32, (taps, wh.shape[2]), 0)
        == lax.broadcasted_iota(jnp.int32, (taps, wh.shape[2]), 1),
        1.0,
        0.0,
    ).astype(BF16)
    lanes = lax.broadcasted_iota(jnp.int32, wh.shape[1:], 1)
    for layer in range(HID):
        value = jnp.dot(hidden_weights[layer], unit, preferred_element_type=F32)
        wh[layer] = (value + extras(bias[:, layer + 1 : layer + 2], lanes, taps)).astype(BF16)
    nodes = ow.shape[0]
    row = out_weights[...].astype(F32)
    row = jnp.concatenate([row] * (LANES // channels), axis=1)
    n = lax.broadcasted_iota(jnp.int32, (nodes, LANES), 0)
    for i in range(ow.shape[1] // LANES):
        m = (lax.broadcasted_iota(jnp.int32, (nodes, LANES), 1) + i * LANES) // channels
        ow[:, i * LANES : (i + 1) * LANES] = jnp.where(m == n, jnp.broadcast_to(row, n.shape), 0.0).astype(BF16)
    pad[0:1, 0 : dither.shape[1]] = dither[...].astype(F32)
    small[0:1, :] = jnp.broadcast_to(out_bias[...], (1, LANES))
    small[1:2, :] = pad[0:1, 0:LANES]


def moved(tiles, by):
    n = len(tiles)
    lanes = lax.broadcasted_iota(jnp.int32, tiles[0].shape, 1)
    turned = [pltpu.roll(v, by % LANES, 1) for v in tiles]
    if by > 0:
        return [turned[0]] + [jnp.where(lanes < by, turned[i - 1], turned[i]) for i in range(1, n)]
    return [jnp.where(lanes >= LANES + by, turned[i + 1], turned[i]) for i in range(n - 1)] + [turned[n - 1]]


def taps_of(tiles, by):
    up, down = moved(tiles, by), moved(tiles, -by)
    return [jnp.concatenate(v, axis=1) for v in (up, tiles, down)]


def deblend(
    total,
    shots,
    pair,
    first,
    second,
    tt1,
    tt2,
    w0,
    wh,
    ow,
    small,
    interference,
    cleaned,
    xn,
    gs,
    zp,
):
    nodes, samples = interference.shape
    windows = samples // LANES + 1
    span = windows * LANES
    window = 2 * LANES
    channels = w0.shape[0]
    rows = nodes * 8
    t, s = lax.axis_index("tm"), lax.axis_index("shot")
    chip = s // 2
    even = chip % 2 == 0
    lowest, highest = chip == 0, chip == shots // 2 - 1
    zero = jnp.zeros((nodes, LANES), F32)
    own_live = []
    for j in range(8):
        if 2 <= j < 4:
            x = pair[j - 2].astype(F32)
            own_live.append(x[:, BEFORE : BEFORE + 1])
        elif j < 6:
            p, q = (second, first) if j < 2 else (first, second)
            x = jnp.where(even, p[j % 2].astype(F32), q[j % 2].astype(F32))
            x = jnp.where(lowest if j < 2 else highest, 0.0, x)
        for w in range(windows):
            xn[pl.ds(w * rows + j, nodes, stride=8), :] = zero if j >= 6 else x[:, w * LANES : (w + 1) * LANES]
            if j >= 6:
                gs[pl.ds(w * rows * 2 + j, nodes, stride=16), :] = zero
                gs[pl.ds(w * rows * 2 + j + 8, nodes, stride=16), :] = zero
    x = [xn[w * rows : (w + 1) * rows, :] for w in range(windows)]
    live = x[BEFORE // LANES][:, BEFORE % LANES : BEFORE % LANES + 1] < LIMIT
    x = [jnp.where(v < LIMIT, v, 0.0).astype(BF16) for v in x] + [jnp.zeros((rows, LANES), BF16)]
    x = jnp.concatenate([jnp.concatenate(x[w : w + 2], axis=1) for w in range(windows)], axis=0)
    sums = [[None] * nodes for _ in range(windows)]
    for a0 in range(0, FN, 2):
        count = min(2, FN - a0)
        y = contract_lanes(x, tt1[a0 * LANES : (a0 + count) * LANES, :])
        for a in range(a0, a0 + count):
            for w in range(windows):
                for n in range(nodes):
                    m = n + a - FN // 2
                    if 0 <= m < nodes:
                        row = w * rows + m * 8
                        v = y[row : row + 8, (a - a0) * LANES : (a - a0 + 1) * LANES]
                        sums[w][n] = v if sums[w][n] is None else sums[w][n] + v
    position = t * samples - LEAD + lax.broadcasted_iota(jnp.int32, (1, span), 1)
    valid = (position >= 0) & (position < total)
    for w in range(windows):
        inside = valid[:, w * LANES : (w + 1) * LANES]
        for n in range(nodes):
            f = jnp.where(live[n * 8 : n * 8 + 8, :] & inside, sums[w][n], 0.0)
            gs[(w * nodes + n) * 16 : (w * nodes + n) * 16 + 8, :] = f.astype(BF16).astype(F32)
    delays = small[1:2, :]
    lane = lax.broadcasted_iota(jnp.int32, (1, LANES), 1)
    own = []
    for j in range(6):
        f = jnp.concatenate([gs[pl.ds(w * rows * 2 + j, nodes, stride=16), :] for w in range(windows)], axis=1)
        if 2 <= j < 4:
            own.append(f)
        shot = jnp.clip(2 * chip - 2 + j, 0, shots - 1)
        delay = jnp.sum(jnp.where(lane == shot, delays, 0.0)).astype(jnp.int32)
        r = jnp.where(valid, pltpu.roll(f, span - delay, 1), 0.0)
        for w in range(windows):
            gs[pl.ds(w * rows * 2 + j + 8, nodes, stride=16), :] = r[:, w * LANES : (w + 1) * LANES]
    row = lax.broadcasted_iota(jnp.int32, (16, span), 0)
    extra = jnp.where(row < 3, 1.0, jnp.where((row == 3) & ~valid, 1.0, 0.0)).astype(BF16)
    acts = []
    for n in range(nodes):
        tiles = [gs[(w * nodes + n) * 16 : (w * nodes + n + 1) * 16, :].astype(BF16) for w in range(windows)]
        columns = jnp.concatenate(taps_of(tiles, 1) + [extra], axis=0)
        act = jnp.dot(w0[...], columns, preferred_element_type=F32)
        acts.append(jnp.maximum(act.astype(BF16), 0.0))
    for layer in range(HID):
        for n in range(nodes):
            tiles = [acts[n][:, w * LANES : (w + 1) * LANES] for w in range(windows)]
            columns = jnp.concatenate(taps_of(tiles, 2 ** (layer + 1)) + [extra], axis=0)
            act = jnp.dot(wh[layer], columns, preferred_element_type=F32)
            acts[n] = jnp.maximum(act.astype(BF16), 0.0)
    pred = jnp.dot(ow[...], jnp.concatenate(acts, axis=0), preferred_element_type=F32) + small[0:1, 0:1]
    pred = pred.astype(BF16).astype(F32)
    odd = s % 2 == 1
    own = jnp.where(odd, own[1], own[0])
    alive = jnp.where(odd, own_live[1], own_live[0]) < LIMIT
    pred = jnp.where(alive & valid, pred, 0.0)
    interference[...] = pltpu.roll(pred, span - LEAD, 1)[:, 0:samples].astype(BF16)
    difference = (own - pred).astype(BF16)
    zp[0:8, :] = jnp.zeros((8, zp.shape[1]), F32)
    zp[nodes + 8 : nodes + 16, :] = jnp.zeros((8, zp.shape[1]), F32)
    for w in range(samples // LANES):
        zp[8 : 8 + nodes, :] = contract_lanes(difference[:, w * LANES : w * LANES + window], tt2[...])
        acc = None
        for a in range(FN):
            v = zp[8 + a - FN // 2 : 8 + a - FN // 2 + nodes, a * LANES : (a + 1) * LANES]
            acc = v if acc is None else acc + v
        cleaned[:, w * LANES : (w + 1) * LANES] = jnp.where(alive, acc, 0.0).astype(BF16)


def local(
    records,
    live,
    dither,
    designature,
    first_weights,
    first_bias,
    hidden_weights,
    hidden_bias,
    out_weights,
    out_bias,
    shaping,
    shots,
    parts,
):
    _, nodes, samples = records.shape
    channels = first_weights.shape[0]
    total = samples * parts
    window = 2 * LANES
    windows = samples // LANES + 1
    span = windows * LANES
    frame = span
    s, t = lax.axis_index("shot"), lax.axis_index("tm")
    time_even, time_odd, partner, pair_even, pair_odd = exchanges(shots, parts)
    send = lambda x, pairs: lax.ppermute(x, AXES, pairs)

    vmem = pl.BlockSpec(memory_space=pltpu.VMEM)
    tt1, tt2, w0, wh, ow, small = pl.pallas_call(
        prepare,
        out_shape=(
            jax.ShapeDtypeStruct((FN * LANES, window), BF16),
            jax.ShapeDtypeStruct((FN * LANES, window), BF16),
            jax.ShapeDtypeStruct((channels, 64), BF16),
            jax.ShapeDtypeStruct((HID, channels, 3 * channels + 16), BF16),
            jax.ShapeDtypeStruct((nodes, nodes * channels), BF16),
            jax.ShapeDtypeStruct((8, LANES), F32),
        ),
        in_specs=[vmem] * 9,
        out_specs=(vmem,) * 6,
        scratch_shapes=[pltpu.VMEM((16, window), F32)],
        compiler_params=pltpu.CompilerParams(vmem_limit_bytes=VMEM_LIMIT),
        cost_estimate=pl.CostEstimate(flops=4 * 10**6, bytes_accessed=10**6, transcendentals=0),
        name="prepare",
    )(
        dither[None],
        designature,
        shaping,
        first_weights.T,
        first_bias[None],
        hidden_weights,
        hidden_bias,
        out_weights[None],
        out_bias[None],
    )

    keep = live[:, :, None] > 0
    dead = jnp.asarray(DEAD, BF16)
    a, b = send(records, time_even), send(records, time_odd)
    mine = lax.optimization_barrier(jnp.where(keep, records, dead))
    t_even = t % 2 == 0
    left = jnp.where(t_even, b, a)[:, :, samples - BEFORE :]
    right = jnp.where(t_even, a, b)[:, :, : frame - BEFORE - samples]
    left = jnp.where(t == 0, jnp.zeros_like(left), left)
    right = jnp.where(t == parts - 1, jnp.zeros_like(right), right)
    x = jnp.concatenate([jnp.where(keep, left, dead), mine, jnp.where(keep, right, dead)], axis=2)
    y = send(x, partner)
    s_even = s % 2 == 0
    pair = jnp.concatenate([jnp.where(s_even, x, y), jnp.where(s_even, y, x)], axis=0)
    first, second = send(pair, pair_even), send(pair, pair_odd)

    interference, cleaned = pl.pallas_call(
        functools.partial(deblend, total, shots),
        out_shape=(jax.ShapeDtypeStruct((nodes, samples), BF16),) * 2,
        in_specs=[vmem] * 9,
        out_specs=(vmem,) * 2,
        scratch_shapes=[
            pltpu.VMEM((windows * nodes * 8, LANES), F32),
            pltpu.VMEM((windows * nodes * 16, LANES), F32),
            pltpu.VMEM((nodes + 16, FN * LANES), F32),
        ],
        compiler_params=pltpu.CompilerParams(vmem_limit_bytes=VMEM_LIMIT),
        cost_estimate=pl.CostEstimate(flops=4 * 10**8, bytes_accessed=10**6, transcendentals=0),
        name="deblend",
    )(pair, first, second, tt1, tt2, w0, wh, ow, small)
    return interference[None], cleaned[None]


def solution(mesh):
    shots, parts = mesh.shape["shot"], mesh.shape["tm"]
    in_specs = (P("shot", None, "tm"), P("shot", None), P(), P(), P(), P(), P(), P(), P(), P(), P())
    out_specs = (P("shot", None, "tm"), P("shot", None, "tm"))
    body = functools.partial(local, shots=shots, parts=parts)
    return jax.shard_map(body, mesh=mesh, in_specs=in_specs, out_specs=out_specs, check_vma=False)
```

```python
import functools

import jax
import jax.numpy as jnp
from jax import lax
from jax.experimental import pallas as pl
from jax.experimental.pallas import tpu as pltpu
from jax.sharding import PartitionSpec as P


HID = 3
FN = 9
FT = 33
SHOT_TAPS = 5
LANES = 128
VMEM_LIMIT = 24 * 2**20
LEAD = 32
BEFORE = LEAD + FT // 2
DEAD = 3e38
LIMIT = 1e38
OFF = 1e30
F32 = jnp.float32
BF16 = jnp.bfloat16
AXES = ("shot", "tm")


def partners(shots, parts, rule):
    out = []
    for s in range(shots):
        for t in range(parts):
            a, b = rule(s, t)
            out.append((s * parts + t, a * parts + b))
    return out


def exchanges(shots, parts):
    def time_odd(s, t):
        o = ((t + 1) ^ 1) - 1
        return (s, o) if 0 <= o < parts else (s ^ 1, t)

    def pair_odd(s, t):
        o = ((s // 2 + 1) ^ 1) - 1
        return (2 * o + s % 2, t) if 0 <= o < shots // 2 else (s ^ 1, t)

    rules = (
        lambda s, t: (s, t ^ 1),
        time_odd,
        lambda s, t: (s ^ 1, t),
        lambda s, t: (s ^ 2, t),
        pair_odd,
    )
    return [partners(shots, parts, rule) for rule in rules]


def contract_lanes(a, b):
    return lax.dot_general(a, b, (((1,), (1,)), ((), ())), preferred_element_type=F32)


def extras(column, lanes, start):
    high = column.astype(BF16).astype(F32)
    middle = (column - high).astype(BF16).astype(F32)
    low = column - high - middle
    out = jnp.where(lanes == start, high, 0.0)
    out = jnp.where(lanes == start + 1, middle, out)
    out = jnp.where(lanes == start + 2, low, out)
    return jnp.where(lanes == start + 3, -OFF, out)


def prepare(
    dither, designature, shaping, first_weights, first_bias, hidden_bias, out_weights, out_bias,
    tt1, tt2, w0, wx, ow, small, pad
):
    window = tt1.shape[1]
    for taps, offset, out in ((designature, 0, tt1), (shaping, LEAD - FT // 2, tt2)):
        pad[...] = jnp.zeros_like(pad)
        pad[0:FN, 0:FT] = taps[...].astype(F32)
        for a in range(FN):
            row = jnp.broadcast_to(pad[a : a + 1, :], (LANES, window))
            row = pltpu.roll(row, offset, 1, stride=1, stride_axis=0)
            out[a * LANES : (a + 1) * LANES, :] = row.astype(BF16)
    channels = out_weights.shape[1]
    pad[...] = jnp.zeros_like(pad)
    pad[0:1, 0:channels] = first_bias[...]
    pad[1 : HID + 1, 0:channels] = hidden_bias[...]
    bias = jnp.transpose(pad[0:8, 0:LANES])[0:channels, :]
    parity = lax.axis_index("shot") % 2
    columns = first_weights.shape[0]
    f = lax.broadcasted_iota(jnp.int32, (columns, w0.shape[1]), 0)
    g = lax.broadcasted_iota(jnp.int32, (columns, w0.shape[1]), 1)
    c, a, k = f // (3 * SHOT_TAPS), (f // 3) % SHOT_TAPS, f % 3
    here = (g // 16 == k) & ((g // 8) % 2 == c) & (g % 8 == a + parity)
    select = jnp.where(here, 1.0, 0.0).astype(BF16)
    value = lax.dot_general(first_weights[...], select, (((0,), (0,)), ((), ())), preferred_element_type=F32)
    lanes = lax.broadcasted_iota(jnp.int32, w0.shape, 1)
    w0[...] = (value + extras(bias[:, 0:1], lanes, 48)).astype(BF16)
    lanes = lax.broadcasted_iota(jnp.int32, wx.shape[1:], 1)
    for layer in range(HID):
        wx[layer] = extras(bias[:, layer + 1 : layer + 2], lanes, 3 * channels).astype(BF16)
    nodes = ow.shape[0]
    row = out_weights[...].astype(F32)
    row = jnp.concatenate([row] * (LANES // channels), axis=1)
    n = lax.broadcasted_iota(jnp.int32, (nodes, LANES), 0)
    for i in range(ow.shape[1] // LANES):
        m = (lax.broadcasted_iota(jnp.int32, (nodes, LANES), 1) + i * LANES) // channels
        ow[:, i * LANES : (i + 1) * LANES] = jnp.where(m == n, jnp.broadcast_to(row, n.shape), 0.0).astype(BF16)
    pad[0:1, 0 : dither.shape[1]] = dither[...].astype(F32)
    small[0:1, :] = jnp.broadcast_to(out_bias[...], (1, LANES))
    small[1:2, :] = pad[0:1, 0:LANES]


def frame_of(parts, even, odd, mine, out):
    t = lax.axis_index("tm")
    samples, span = mine.shape[2], out.shape[2]
    x = mine[0].astype(F32)
    alive = x[:, 0:1] < LIMIT
    a, b = even[0].astype(F32), odd[0].astype(F32)
    is_even = t % 2 == 0
    left = jnp.where(t == 0, 0.0, jnp.where(is_even, b, a))
    right = jnp.where(t == parts - 1, 0.0, jnp.where(is_even, a, b))
    left, right = jnp.where(alive, left, DEAD), jnp.where(alive, right, DEAD)
    gap = jnp.zeros((x.shape[0], span - samples), F32)
    lanes = lax.broadcasted_iota(jnp.int32, (x.shape[0], span), 1)
    spread = [jnp.concatenate([v, gap], axis=1) for v in (left, x, right)]
    left = pltpu.roll(spread[0], span + BEFORE - samples, 1)
    x, right = pltpu.roll(spread[1], BEFORE, 1), pltpu.roll(spread[2], (BEFORE + samples) % span, 1)
    x = jnp.where(lanes < BEFORE, left, jnp.where(lanes < BEFORE + samples, x, right))
    out[0] = x.astype(BF16)


def moved(tiles, by):
    n = len(tiles)
    lanes = lax.broadcasted_iota(jnp.int32, tiles[0].shape, 1)
    turned = [pltpu.roll(v, by % LANES, 1) for v in tiles]
    if by > 0:
        return [turned[0]] + [jnp.where(lanes < by, turned[i - 1], turned[i]) for i in range(1, n)]
    return [jnp.where(lanes >= LANES + by, turned[i + 1], turned[i]) for i in range(n - 1)] + [turned[n - 1]]


def taps_of(tiles, by):
    up, down = moved(tiles, by), moved(tiles, -by)
    return [jnp.concatenate(v, axis=1) for v in (up, tiles, down)]


def deblend(
    total,
    shots,
    pair,
    first,
    second,
    tt1,
    tt2,
    w0,
    hidden,
    wx,
    ow,
    small,
    interference,
    cleaned,
    xn,
    gs,
    zp,
    wh,
):
    nodes, samples = interference.shape
    windows = samples // LANES + 1
    span = windows * LANES
    window = 2 * LANES
    rows = nodes * 8
    t, s = lax.axis_index("tm"), lax.axis_index("shot")
    chip = s // 2
    even = chip % 2 == 0
    lowest, highest = chip == 0, chip == shots // 2 - 1
    zero = jnp.zeros((nodes, LANES), F32)
    depth = hidden.shape[2]
    wh[...] = wx[...]
    wh[:, :, 0:depth] = hidden[...]
    odd = s % 2 == 1
    alive = pair[0].astype(F32)[:, BEFORE : BEFORE + 1] < LIMIT
    near = [[jnp.where(odd, v[1 - j].astype(F32), v[j].astype(F32)) for j in range(2)] for v in (pair, first, second)]
    for j in range(8):
        if 2 <= j < 4:
            x = near[0][j - 2]
        elif j < 6:
            p, q = (2, 1) if j < 2 else (1, 2)
            x = jnp.where(even, near[p][j % 2], near[q][j % 2])
            x = jnp.where(lowest if j < 2 else highest, 0.0, x)
        for w in range(windows):
            xn[pl.ds(w * rows + j, nodes, stride=8), :] = zero if j >= 6 else x[:, w * LANES : (w + 1) * LANES]
            if j >= 6:
                gs[pl.ds(w * rows * 2 + j, nodes, stride=16), :] = zero
                gs[pl.ds(w * rows * 2 + j + 8, nodes, stride=16), :] = zero
    x = [xn[w * rows : (w + 1) * rows, :] for w in range(windows)]
    live = x[BEFORE // LANES][:, BEFORE % LANES : BEFORE % LANES + 1] < LIMIT
    x = [jnp.where(v < LIMIT, v, 0.0).astype(BF16) for v in x] + [jnp.zeros((rows, LANES), BF16)]
    x = jnp.concatenate([jnp.concatenate(x[w : w + 2], axis=1) for w in range(windows)], axis=0)
    sums = [[None] * nodes for _ in range(windows)]
    for a0 in range(0, FN, 2):
        count = min(2, FN - a0)
        y = contract_lanes(x, tt1[a0 * LANES : (a0 + count) * LANES, :])
        for a in range(a0, a0 + count):
            for w in range(windows):
                for n in range(nodes):
                    m = n + a - FN // 2
                    if 0 <= m < nodes:
                        row = w * rows + m * 8
                        v = y[row : row + 8, (a - a0) * LANES : (a - a0 + 1) * LANES]
                        sums[w][n] = v if sums[w][n] is None else sums[w][n] + v
    position = t * samples - LEAD + lax.broadcasted_iota(jnp.int32, (1, span), 1)
    valid = (position >= 0) & (position < total)
    for w in range(windows):
        inside = valid[:, w * LANES : (w + 1) * LANES]
        for n in range(nodes):
            f = jnp.where(live[n * 8 : n * 8 + 8, :] & inside, sums[w][n], 0.0)
            gs[(w * nodes + n) * 16 : (w * nodes + n) * 16 + 8, :] = f.astype(BF16).astype(F32)
    delays = small[1:2, :]
    lane = lax.broadcasted_iota(jnp.int32, (1, LANES), 1)
    own = []
    for j in range(6):
        f = jnp.concatenate([gs[pl.ds(w * rows * 2 + j, nodes, stride=16), :] for w in range(windows)], axis=1)
        if 2 <= j < 4:
            own.append(f)
        shot = jnp.clip(2 * chip - 2 + j, 0, shots - 1)
        delay = jnp.sum(jnp.where(lane == shot, delays, 0.0)).astype(jnp.int32)
        r = jnp.where(valid, pltpu.roll(f, span - delay, 1), 0.0)
        for w in range(windows):
            gs[pl.ds(w * rows * 2 + j + 8, nodes, stride=16), :] = r[:, w * LANES : (w + 1) * LANES]
    row = lax.broadcasted_iota(jnp.int32, (16, span), 0)
    extra = jnp.where(row < 3, 1.0, jnp.where((row == 3) & ~valid, 1.0, 0.0)).astype(BF16)
    acts = []
    for n in range(nodes):
        tiles = [gs[(w * nodes + n) * 16 : (w * nodes + n + 1) * 16, :].astype(BF16) for w in range(windows)]
        columns = jnp.concatenate(taps_of(tiles, 1) + [extra], axis=0)
        act = jnp.dot(w0[...], columns, preferred_element_type=F32)
        acts.append(jnp.maximum(act.astype(BF16), 0.0))
    for layer in range(HID):
        for n in range(nodes):
            tiles = [acts[n][:, w * LANES : (w + 1) * LANES] for w in range(windows)]
            columns = jnp.concatenate(taps_of(tiles, 2 ** (layer + 1)) + [extra], axis=0)
            act = jnp.dot(wh[layer][:, 0 : depth + 16], columns, preferred_element_type=F32)
            acts[n] = jnp.maximum(act.astype(BF16), 0.0)
    pred = jnp.dot(ow[...], jnp.concatenate(acts, axis=0), preferred_element_type=F32) + small[0:1, 0:1]
    pred = pred.astype(BF16).astype(F32)
    own = jnp.where(odd, own[1], own[0])
    pred = jnp.where(alive & valid, pred, 0.0)
    interference[...] = pltpu.roll(pred, span - LEAD, 1)[:, 0:samples].astype(BF16)
    difference = (own - pred).astype(BF16)
    zp[0:8, :] = jnp.zeros((8, zp.shape[1]), F32)
    zp[nodes + 8 : nodes + 16, :] = jnp.zeros((8, zp.shape[1]), F32)
    for w in range(samples // LANES):
        zp[8 : 8 + nodes, :] = contract_lanes(difference[:, w * LANES : w * LANES + window], tt2[...])
        acc = None
        for a in range(FN):
            v = zp[8 + a - FN // 2 : 8 + a - FN // 2 + nodes, a * LANES : (a + 1) * LANES]
            acc = v if acc is None else acc + v
        cleaned[:, w * LANES : (w + 1) * LANES] = jnp.where(alive, acc, 0.0).astype(BF16)


def local(
    records,
    live,
    dither,
    designature,
    first_weights,
    first_bias,
    hidden_weights,
    hidden_bias,
    out_weights,
    out_bias,
    shaping,
    shots,
    parts,
):
    _, nodes, samples = records.shape
    channels = first_weights.shape[0]
    total = samples * parts
    window = 2 * LANES
    windows = samples // LANES + 1
    span = windows * LANES
    time_even, time_odd, partner, pair_even, pair_odd = exchanges(shots, parts)

    def send(x, pairs):
        return lax.ppermute(x, AXES, pairs)


    vmem = pl.BlockSpec(memory_space=pltpu.VMEM)
    tt1, tt2, w0, wx, ow, small = pl.pallas_call(
        prepare,
        out_shape=(
            jax.ShapeDtypeStruct((FN * LANES, window), BF16),
            jax.ShapeDtypeStruct((FN * LANES, window), BF16),
            jax.ShapeDtypeStruct((channels, 64), BF16),
            jax.ShapeDtypeStruct((HID, channels, window), BF16),
            jax.ShapeDtypeStruct((nodes, nodes * channels), BF16),
            jax.ShapeDtypeStruct((8, LANES), F32),
        ),
        in_specs=[vmem] * 8,
        out_specs=(vmem,) * 6,
        scratch_shapes=[pltpu.VMEM((16, window), F32)],
        compiler_params=pltpu.CompilerParams(vmem_limit_bytes=VMEM_LIMIT),
        cost_estimate=pl.CostEstimate(flops=10**8, bytes_accessed=10**7, transcendentals=0),
        name="prepare",
    )(
        dither[None],
        designature,
        shaping,
        first_weights.T,
        first_bias[None],
        hidden_bias,
        out_weights[None],
        out_bias[None],
    )

    keep = live[:, :, None] > 0
    dead = jnp.asarray(DEAD, BF16)
    a, b = send(records, time_even), send(records, time_odd)
    mine = lax.optimization_barrier(jnp.where(keep, records, dead))
    x = pl.pallas_call(
        functools.partial(frame_of, parts),
        out_shape=jax.ShapeDtypeStruct((1, nodes, span), BF16),
        in_specs=[vmem] * 3,
        out_specs=vmem,
        compiler_params=pltpu.CompilerParams(vmem_limit_bytes=VMEM_LIMIT),
        name="frame",
    )(a, b, mine)
    pair = jnp.concatenate([x, send(x, partner)], axis=0)
    first, second = send(pair, pair_even), send(pair, pair_odd)

    interference, cleaned = pl.pallas_call(
        functools.partial(deblend, total, shots),
        out_shape=(jax.ShapeDtypeStruct((nodes, samples), BF16),) * 2,
        in_specs=[vmem] * 10,
        out_specs=(vmem,) * 2,
        scratch_shapes=[
            pltpu.VMEM((windows * nodes * 8, LANES), F32),
            pltpu.VMEM((windows * nodes * 16, LANES), F32),
            pltpu.VMEM((nodes + 16, FN * LANES), F32),
            pltpu.VMEM((HID, channels, window), BF16),
        ],
        compiler_params=pltpu.CompilerParams(vmem_limit_bytes=VMEM_LIMIT),
        cost_estimate=pl.CostEstimate(flops=4 * 10**8, bytes_accessed=10**6, transcendentals=0),
        name="deblend",
    )(pair, first, second, tt1, tt2, w0, hidden_weights, wx, ow, small)
    return interference[None], cleaned[None]


def solution(mesh):
    shots, parts = mesh.shape["shot"], mesh.shape["tm"]
    in_specs = (P("shot", None, "tm"), P("shot", None), P(), P(), P(), P(), P(), P(), P(), P(), P())
    out_specs = (P("shot", None, "tm"), P("shot", None, "tm"))

    def body(*args):
        return local(*args, shots=shots, parts=parts)

    return jax.shard_map(body, mesh=mesh, in_specs=in_specs, out_specs=out_specs, check_vma=False)
```

```python
import functools

import jax
import jax.numpy as jnp
from jax import lax
from jax.experimental import pallas as pl
from jax.experimental.pallas import tpu as pltpu
from jax.sharding import PartitionSpec as P


HID = 3
FN = 9
FT = 33
SHOT_TAPS = 5
LANES = 128
VMEM_LIMIT = 24 * 2**20
LEAD = 32
BEFORE = LEAD + FT // 2
DEAD = 3e38
LIMIT = 1e38
OFF = 1e30
F32 = jnp.float32
BF16 = jnp.bfloat16
AXES = ("shot", "tm")


def partners(shots, parts, rule):
    out = []
    for s in range(shots):
        for t in range(parts):
            a, b = rule(s, t)
            out.append((s * parts + t, a * parts + b))
    return out


def exchanges(shots, parts):
    def meet(i, n, k):
        if i % 3 == k and i + 1 < n:
            return i + 1
        return i - 1 if i % 3 == (k + 1) % 3 and i > 0 else i

    def along_time(s, t, k):
        o = meet(t, parts, k)
        return (s ^ 1, t) if o == t else (s, o)

    def along_shot(s, t, k):
        o = meet(s // 2, shots // 2, k)
        return (s ^ 1, t) if o == s // 2 else (2 * o + s % 2, t)

    times = [partners(shots, parts, functools.partial(along_time, k=k)) for k in range(3)]
    pairs = [partners(shots, parts, functools.partial(along_shot, k=k)) for k in range(3)]
    return times, partners(shots, parts, lambda s, t: (s ^ 1, t)), pairs


def pick(index, values):
    return jnp.where(index == 0, values[0], jnp.where(index == 1, values[1], values[2]))


def contract_lanes(a, b):
    return lax.dot_general(a, b, (((1,), (1,)), ((), ())), preferred_element_type=F32)


def extras(column, lanes, start):
    high = column.astype(BF16).astype(F32)
    middle = (column - high).astype(BF16).astype(F32)
    low = column - high - middle
    out = jnp.where(lanes == start, high, 0.0)
    out = jnp.where(lanes == start + 1, middle, out)
    out = jnp.where(lanes == start + 2, low, out)
    return jnp.where(lanes == start + 3, -OFF, out)


def prepare(
    dither, designature, shaping, first_weights, first_bias, hidden_bias, out_weights, out_bias,
    tt1, tt2, w0, wx, ow, small, pad
):
    window = tt1.shape[1]
    for taps, offset, out in ((designature, 0, tt1), (shaping, LEAD - FT // 2, tt2)):
        pad[...] = jnp.zeros_like(pad)
        pad[0:FN, 0:FT] = taps[...].astype(F32)
        for a in range(FN):
            row = jnp.broadcast_to(pad[a : a + 1, :], (LANES, window))
            row = pltpu.roll(row, offset, 1, stride=1, stride_axis=0)
            out[a * LANES : (a + 1) * LANES, :] = row.astype(BF16)
    channels = out_weights.shape[1]
    pad[...] = jnp.zeros_like(pad)
    pad[0:1, 0:channels] = first_bias[...]
    pad[1 : HID + 1, 0:channels] = hidden_bias[...]
    bias = jnp.transpose(pad[0:8, 0:LANES])[0:channels, :]
    parity = lax.axis_index("shot") % 2
    columns = first_weights.shape[0]
    f = lax.broadcasted_iota(jnp.int32, (columns, w0.shape[1]), 0)
    g = lax.broadcasted_iota(jnp.int32, (columns, w0.shape[1]), 1)
    c, a, k = f // (3 * SHOT_TAPS), (f // 3) % SHOT_TAPS, f % 3
    here = (g // 16 == k) & ((g // 8) % 2 == c) & (g % 8 == a + parity)
    select = jnp.where(here, 1.0, 0.0).astype(BF16)
    value = lax.dot_general(first_weights[...], select, (((0,), (0,)), ((), ())), preferred_element_type=F32)
    lanes = lax.broadcasted_iota(jnp.int32, w0.shape, 1)
    w0[...] = (value + extras(bias[:, 0:1], lanes, 48)).astype(BF16)
    lanes = lax.broadcasted_iota(jnp.int32, wx.shape[1:], 1)
    for layer in range(HID):
        wx[layer] = extras(bias[:, layer + 1 : layer + 2], lanes, 3 * channels).astype(BF16)
    nodes = ow.shape[0]
    row = out_weights[...].astype(F32)
    row = jnp.concatenate([row] * (LANES // channels), axis=1)
    n = lax.broadcasted_iota(jnp.int32, (nodes, LANES), 0)
    for i in range(ow.shape[1] // LANES):
        m = (lax.broadcasted_iota(jnp.int32, (nodes, LANES), 1) + i * LANES) // channels
        ow[:, i * LANES : (i + 1) * LANES] = jnp.where(m == n, jnp.broadcast_to(row, n.shape), 0.0).astype(BF16)
    pad[0:1, 0 : dither.shape[1]] = dither[...].astype(F32)
    small[0:1, :] = jnp.broadcast_to(out_bias[...], (1, LANES))
    small[1:2, :] = pad[0:1, 0:LANES]


def frame_of(parts, first, second, third, mine, out):
    t = lax.axis_index("tm")
    samples, span = mine.shape[2], out.shape[2]
    x = mine[0].astype(F32)
    alive = x[:, 0:1] < LIMIT
    got = [v[0].astype(F32) for v in (first, second, third)]
    left = jnp.where(t == 0, 0.0, pick((t + 2) % 3, got))
    right = jnp.where(t == parts - 1, 0.0, pick(t % 3, got))
    left, right = jnp.where(alive, left, DEAD), jnp.where(alive, right, DEAD)
    gap = jnp.zeros((x.shape[0], span - samples), F32)
    lanes = lax.broadcasted_iota(jnp.int32, (x.shape[0], span), 1)
    spread = [jnp.concatenate([v, gap], axis=1) for v in (left, x, right)]
    left = pltpu.roll(spread[0], span + BEFORE - samples, 1)
    x, right = pltpu.roll(spread[1], BEFORE, 1), pltpu.roll(spread[2], (BEFORE + samples) % span, 1)
    x = jnp.where(lanes < BEFORE, left, jnp.where(lanes < BEFORE + samples, x, right))
    out[0] = x.astype(BF16)


def moved(tiles, by):
    n = len(tiles)
    lanes = lax.broadcasted_iota(jnp.int32, tiles[0].shape, 1)
    turned = [pltpu.roll(v, by % LANES, 1) for v in tiles]
    if by > 0:
        return [turned[0]] + [jnp.where(lanes < by, turned[i - 1], turned[i]) for i in range(1, n)]
    return [jnp.where(lanes >= LANES + by, turned[i + 1], turned[i]) for i in range(n - 1)] + [turned[n - 1]]


def taps_of(tiles, by):
    up, down = moved(tiles, by), moved(tiles, -by)
    return [jnp.concatenate(v, axis=1) for v in (up, tiles, down)]


def deblend(
    total,
    shots,
    pair,
    first,
    second,
    third,
    tt1,
    tt2,
    w0,
    hidden,
    wx,
    ow,
    small,
    interference,
    cleaned,
    xn,
    gs,
    zp,
    wh,
):
    nodes, samples = interference.shape
    windows = samples // LANES + 1
    span = windows * LANES
    window = 2 * LANES
    rows = nodes * 8
    t, s = lax.axis_index("tm"), lax.axis_index("shot")
    chip = s // 2
    lowest, highest = chip == 0, chip == shots // 2 - 1
    zero = jnp.zeros((nodes, LANES), F32)
    depth = hidden.shape[2]
    wh[...] = wx[...]
    wh[:, :, 0:depth] = hidden[...]
    odd = s % 2 == 1
    alive = pair[0].astype(F32)[:, BEFORE : BEFORE + 1] < LIMIT
    near = [[jnp.where(odd, v[1 - j].astype(F32), v[j].astype(F32)) for j in range(2)] for v in (pair, first, second, third)]
    for j in range(8):
        if 2 <= j < 4:
            x = near[0][j - 2]
        elif j < 6:
            turn = (chip + 2) % 3 if j < 2 else chip % 3
            x = pick(turn, [v[j % 2] for v in near[1:]])
            x = jnp.where(lowest if j < 2 else highest, 0.0, x)
        for w in range(windows):
            xn[pl.ds(w * rows + j, nodes, stride=8), :] = zero if j >= 6 else x[:, w * LANES : (w + 1) * LANES]
            if j >= 6:
                gs[pl.ds(w * rows * 2 + j, nodes, stride=16), :] = zero
                gs[pl.ds(w * rows * 2 + j + 8, nodes, stride=16), :] = zero
    x = [xn[w * rows : (w + 1) * rows, :] for w in range(windows)]
    live = x[BEFORE // LANES][:, BEFORE % LANES : BEFORE % LANES + 1] < LIMIT
    x = [jnp.where(v < LIMIT, v, 0.0).astype(BF16) for v in x] + [jnp.zeros((rows, LANES), BF16)]
    x = jnp.concatenate([jnp.concatenate(x[w : w + 2], axis=1) for w in range(windows)], axis=0)
    sums = [[None] * nodes for _ in range(windows)]
    for a0 in range(0, FN, 2):
        count = min(2, FN - a0)
        y = contract_lanes(x, tt1[a0 * LANES : (a0 + count) * LANES, :])
        for a in range(a0, a0 + count):
            for w in range(windows):
                for n in range(nodes):
                    m = n + a - FN // 2
                    if 0 <= m < nodes:
                        row = w * rows + m * 8
                        v = y[row : row + 8, (a - a0) * LANES : (a - a0 + 1) * LANES]
                        sums[w][n] = v if sums[w][n] is None else sums[w][n] + v
    position = t * samples - LEAD + lax.broadcasted_iota(jnp.int32, (1, span), 1)
    valid = (position >= 0) & (position < total)
    for w in range(windows):
        inside = valid[:, w * LANES : (w + 1) * LANES]
        for n in range(nodes):
            f = jnp.where(live[n * 8 : n * 8 + 8, :] & inside, sums[w][n], 0.0)
            gs[(w * nodes + n) * 16 : (w * nodes + n) * 16 + 8, :] = f.astype(BF16).astype(F32)
    delays = small[1:2, :]
    lane = lax.broadcasted_iota(jnp.int32, (1, LANES), 1)
    own = []
    for j in range(6):
        f = jnp.concatenate([gs[pl.ds(w * rows * 2 + j, nodes, stride=16), :] for w in range(windows)], axis=1)
        if 2 <= j < 4:
            own.append(f)
        shot = jnp.clip(2 * chip - 2 + j, 0, shots - 1)
        delay = jnp.sum(jnp.where(lane == shot, delays, 0.0)).astype(jnp.int32)
        r = jnp.where(valid, pltpu.roll(f, span - delay, 1), 0.0)
        for w in range(windows):
            gs[pl.ds(w * rows * 2 + j + 8, nodes, stride=16), :] = r[:, w * LANES : (w + 1) * LANES]
    row = lax.broadcasted_iota(jnp.int32, (16, span), 0)
    extra = jnp.where(row < 3, 1.0, jnp.where((row == 3) & ~valid, 1.0, 0.0)).astype(BF16)
    acts = []
    for n in range(nodes):
        tiles = [gs[(w * nodes + n) * 16 : (w * nodes + n + 1) * 16, :].astype(BF16) for w in range(windows)]
        columns = jnp.concatenate(taps_of(tiles, 1) + [extra], axis=0)
        act = jnp.dot(w0[...], columns, preferred_element_type=F32)
        acts.append(jnp.maximum(act.astype(BF16), 0.0))
    for layer in range(HID):
        for n in range(nodes):
            tiles = [acts[n][:, w * LANES : (w + 1) * LANES] for w in range(windows)]
            columns = jnp.concatenate(taps_of(tiles, 2 ** (layer + 1)) + [extra], axis=0)
            act = jnp.dot(wh[layer][:, 0 : depth + 16], columns, preferred_element_type=F32)
            acts[n] = jnp.maximum(act.astype(BF16), 0.0)
    pred = jnp.dot(ow[...], jnp.concatenate(acts, axis=0), preferred_element_type=F32) + small[0:1, 0:1]
    pred = pred.astype(BF16).astype(F32)
    own = jnp.where(odd, own[1], own[0])
    pred = jnp.where(alive & valid, pred, 0.0)
    interference[...] = pltpu.roll(pred, span - LEAD, 1)[:, 0:samples].astype(BF16)
    difference = (own - pred).astype(BF16)
    zp[0:8, :] = jnp.zeros((8, zp.shape[1]), F32)
    zp[nodes + 8 : nodes + 16, :] = jnp.zeros((8, zp.shape[1]), F32)
    for w in range(samples // LANES):
        zp[8 : 8 + nodes, :] = contract_lanes(difference[:, w * LANES : w * LANES + window], tt2[...])
        acc = None
        for a in range(FN):
            v = zp[8 + a - FN // 2 : 8 + a - FN // 2 + nodes, a * LANES : (a + 1) * LANES]
            acc = v if acc is None else acc + v
        cleaned[:, w * LANES : (w + 1) * LANES] = jnp.where(alive, acc, 0.0).astype(BF16)


def local(
    records,
    live,
    dither,
    designature,
    first_weights,
    first_bias,
    hidden_weights,
    hidden_bias,
    out_weights,
    out_bias,
    shaping,
    shots,
    parts,
):
    _, nodes, samples = records.shape
    channels = first_weights.shape[0]
    total = samples * parts
    window = 2 * LANES
    windows = samples // LANES + 1
    span = windows * LANES
    times, partner, pairs = exchanges(shots, parts)

    def send(x, pairs):
        return lax.ppermute(x, AXES, pairs)


    vmem = pl.BlockSpec(memory_space=pltpu.VMEM)
    tt1, tt2, w0, wx, ow, small = pl.pallas_call(
        prepare,
        out_shape=(
            jax.ShapeDtypeStruct((FN * LANES, window), BF16),
            jax.ShapeDtypeStruct((FN * LANES, window), BF16),
            jax.ShapeDtypeStruct((channels, 64), BF16),
            jax.ShapeDtypeStruct((HID, channels, window), BF16),
            jax.ShapeDtypeStruct((nodes, nodes * channels), BF16),
            jax.ShapeDtypeStruct((8, LANES), F32),
        ),
        in_specs=[vmem] * 8,
        out_specs=(vmem,) * 6,
        scratch_shapes=[pltpu.VMEM((16, window), F32)],
        compiler_params=pltpu.CompilerParams(vmem_limit_bytes=VMEM_LIMIT),
        cost_estimate=pl.CostEstimate(flops=10**8, bytes_accessed=10**7, transcendentals=0),
        name="prepare",
    )(
        dither[None],
        designature,
        shaping,
        first_weights.T,
        first_bias[None],
        hidden_bias,
        out_weights[None],
        out_bias[None],
    )

    keep = live[:, :, None] > 0
    dead = jnp.asarray(DEAD, BF16)
    around = [send(records, times[k]) for k in range(3)]
    mine = lax.optimization_barrier(jnp.where(keep, records, dead))
    x = pl.pallas_call(
        functools.partial(frame_of, parts),
        out_shape=jax.ShapeDtypeStruct((1, nodes, span), BF16),
        in_specs=[vmem] * 4,
        out_specs=vmem,
        compiler_params=pltpu.CompilerParams(vmem_limit_bytes=VMEM_LIMIT),
        name="frame",
    )(*around, mine)
    pair = jnp.concatenate([x, send(x, partner)], axis=0)
    near = [send(pair, pairs[k]) for k in range(3)]

    interference, cleaned = pl.pallas_call(
        functools.partial(deblend, total, shots),
        out_shape=(jax.ShapeDtypeStruct((nodes, samples), BF16),) * 2,
        in_specs=[vmem] * 11,
        out_specs=(vmem,) * 2,
        scratch_shapes=[
            pltpu.VMEM((windows * nodes * 8, LANES), F32),
            pltpu.VMEM((windows * nodes * 16, LANES), F32),
            pltpu.VMEM((nodes + 16, FN * LANES), F32),
            pltpu.VMEM((HID, channels, window), BF16),
        ],
        compiler_params=pltpu.CompilerParams(vmem_limit_bytes=VMEM_LIMIT),
        cost_estimate=pl.CostEstimate(flops=4 * 10**8, bytes_accessed=10**6, transcendentals=0),
        name="deblend",
    )(pair, *near, tt1, tt2, w0, hidden_weights, wx, ow, small)
    return interference[None], cleaned[None]


def solution(mesh):
    shots, parts = mesh.shape["shot"], mesh.shape["tm"]
    in_specs = (P("shot", None, "tm"), P("shot", None), P(), P(), P(), P(), P(), P(), P(), P(), P())
    out_specs = (P("shot", None, "tm"), P("shot", None, "tm"))

    def body(*args):
        return local(*args, shots=shots, parts=parts)

    return jax.shard_map(body, mesh=mesh, in_specs=in_specs, out_specs=out_specs, check_vma=False)
```

```python
import functools

import jax
import jax.numpy as jnp
from jax import lax
from jax.experimental import pallas as pl
from jax.experimental.pallas import tpu as pltpu
from jax.sharding import PartitionSpec as P


HID = 3
FN = 9
FT = 33
SHOT_TAPS = 5
LANES = 128
VMEM_LIMIT = 24 * 2**20
LEAD = 32
BEFORE = LEAD + FT // 2
DEAD = 3e38
LIMIT = 1e38
OFF = 1e30
F32 = jnp.float32
BF16 = jnp.bfloat16
AXES = ("shot", "tm")


def partners(shots, parts, rule):
    out = []
    for s in range(shots):
        for t in range(parts):
            a, b = rule(s, t)
            out.append((s * parts + t, a * parts + b))
    return out


def exchanges(shots, parts):
    def meet(i, n, k):
        if i % 3 == k and i + 1 < n:
            return i + 1
        return i - 1 if i % 3 == (k + 1) % 3 and i > 0 else i

    def along_time(s, t, k):
        o = meet(t, parts, k)
        return (s ^ 1, t) if o == t else (s, o)

    def along_shot(s, t, k):
        o = meet(s // 2, shots // 2, k)
        return (s ^ 1, t) if o == s // 2 else (2 * o + s % 2, t)

    times = [partners(shots, parts, functools.partial(along_time, k=k)) for k in range(3)]
    pairs = [partners(shots, parts, functools.partial(along_shot, k=k)) for k in range(3)]
    return times, partners(shots, parts, lambda s, t: (s ^ 1, t)), pairs


def pick(index, values):
    return jnp.where(index == 0, values[0], jnp.where(index == 1, values[1], values[2]))


def contract_lanes(a, b):
    return lax.dot_general(a, b, (((1,), (1,)), ((), ())), preferred_element_type=F32)


def extras(column, lanes, start):
    high = column.astype(BF16).astype(F32)
    middle = (column - high).astype(BF16).astype(F32)
    low = column - high - middle
    out = jnp.where(lanes == start, high, 0.0)
    out = jnp.where(lanes == start + 1, middle, out)
    out = jnp.where(lanes == start + 2, low, out)
    return jnp.where(lanes == start + 3, -OFF, out)


def prepare(
    dither, designature, shaping, first_weights, first_bias, hidden_bias, out_weights, out_bias,
    tt1, tt2, w0, wx, ow, small, pad
):
    window = tt1.shape[1]
    for taps, offset, out in ((designature, 0, tt1), (shaping, LEAD - FT // 2, tt2)):
        pad[...] = jnp.zeros_like(pad)
        pad[0:FN, 0:FT] = taps[...].astype(F32)
        for a in range(FN):
            row = jnp.broadcast_to(pad[a : a + 1, :], (LANES, window))
            row = pltpu.roll(row, offset, 1, stride=1, stride_axis=0)
            out[a * LANES : (a + 1) * LANES, :] = row.astype(BF16)
    channels = out_weights.shape[1]
    pad[...] = jnp.zeros_like(pad)
    pad[0:1, 0:channels] = first_bias[...]
    pad[1 : HID + 1, 0:channels] = hidden_bias[...]
    bias = jnp.transpose(pad[0:8, 0:LANES])[0:channels, :]
    parity = lax.axis_index("shot") % 2
    columns = first_weights.shape[0]
    f = lax.broadcasted_iota(jnp.int32, (columns, w0.shape[1]), 0)
    g = lax.broadcasted_iota(jnp.int32, (columns, w0.shape[1]), 1)
    c, a, k = f // (3 * SHOT_TAPS), (f // 3) % SHOT_TAPS, f % 3
    here = (g // 16 == k) & ((g // 8) % 2 == c) & (g % 8 == a + parity)
    select = jnp.where(here, 1.0, 0.0).astype(BF16)
    value = lax.dot_general(first_weights[...], select, (((0,), (0,)), ((), ())), preferred_element_type=F32)
    lanes = lax.broadcasted_iota(jnp.int32, w0.shape, 1)
    w0[...] = (value + extras(bias[:, 0:1], lanes, 48)).astype(BF16)
    lanes = lax.broadcasted_iota(jnp.int32, wx.shape[1:], 1)
    for layer in range(HID):
        wx[layer] = extras(bias[:, layer + 1 : layer + 2], lanes, 3 * channels).astype(BF16)
    nodes = ow.shape[0]
    row = out_weights[...].astype(F32)
    row = jnp.concatenate([row] * (LANES // channels), axis=1)
    n = lax.broadcasted_iota(jnp.int32, (nodes, LANES), 0)
    for i in range(ow.shape[1] // LANES):
        m = (lax.broadcasted_iota(jnp.int32, (nodes, LANES), 1) + i * LANES) // channels
        ow[:, i * LANES : (i + 1) * LANES] = jnp.where(m == n, jnp.broadcast_to(row, n.shape), 0.0).astype(BF16)
    pad[0:1, 0 : dither.shape[1]] = dither[...].astype(F32)
    small[0:1, :] = jnp.broadcast_to(out_bias[...], (1, LANES))
    small[1:2, :] = pad[0:1, 0:LANES]


def frame_of(parts, first, second, third, mine, out):
    t = lax.axis_index("tm")
    samples, span = mine.shape[2], out.shape[2]
    x = mine[0].astype(F32)
    alive = x[:, 0:1] < LIMIT
    got = [v[0].astype(F32) for v in (first, second, third)]
    left = jnp.where(t == 0, 0.0, pick((t + 2) % 3, got))
    right = jnp.where(t == parts - 1, 0.0, pick(t % 3, got))
    left, right = jnp.where(alive, left, DEAD), jnp.where(alive, right, DEAD)
    tiles = [left[:, samples - LANES :]] + [x[:, v : v + LANES] for v in range(0, samples, LANES)] + [right[:, 0:LANES]]
    turned = [pltpu.roll(v, BEFORE, 1) for v in tiles]
    ahead = lax.broadcasted_iota(jnp.int32, tiles[0].shape, 1) < BEFORE
    for w in range(span // LANES):
        out[0, :, w * LANES : (w + 1) * LANES] = jnp.where(ahead, turned[w], turned[w + 1]).astype(BF16)


def moved(tiles, by):
    n = len(tiles)
    lanes = lax.broadcasted_iota(jnp.int32, tiles[0].shape, 1)
    turned = [pltpu.roll(v, by % LANES, 1) for v in tiles]
    if by > 0:
        return [turned[0]] + [jnp.where(lanes < by, turned[i - 1], turned[i]) for i in range(1, n)]
    return [jnp.where(lanes >= LANES + by, turned[i + 1], turned[i]) for i in range(n - 1)] + [turned[n - 1]]


def taps_of(tiles, by):
    up, down = moved(tiles, by), moved(tiles, -by)
    return [jnp.concatenate(v, axis=1) for v in (up, tiles, down)]


def deblend(
    total,
    shots,
    pair,
    first,
    second,
    third,
    tt1,
    tt2,
    w0,
    hidden,
    wx,
    ow,
    small,
    interference,
    cleaned,
    xn,
    gs,
    zp,
    wh,
):
    nodes, samples = interference.shape
    windows = samples // LANES + 1
    span = windows * LANES
    window = 2 * LANES
    rows = nodes * 8
    t, s = lax.axis_index("tm"), lax.axis_index("shot")
    chip = s // 2
    lowest, highest = chip == 0, chip == shots // 2 - 1
    zero = jnp.zeros((nodes, LANES), F32)
    depth = hidden.shape[2]
    odd = s % 2 == 1
    alive = pair[0].astype(F32)[:, BEFORE : BEFORE + 1] < LIMIT
    near = [[jnp.where(odd, v[1 - j].astype(F32), v[j].astype(F32)) for j in range(2)] for v in (pair, first, second, third)]
    for j in range(8):
        if 2 <= j < 4:
            x = near[0][j - 2]
        elif j < 6:
            turn = (chip + 2) % 3 if j < 2 else chip % 3
            x = pick(turn, [v[j % 2] for v in near[1:]])
            x = jnp.where(lowest if j < 2 else highest, 0.0, x)
        for w in range(windows):
            xn[pl.ds(w * rows + j, nodes, stride=8), :] = zero if j >= 6 else x[:, w * LANES : (w + 1) * LANES]
            if j >= 6:
                gs[pl.ds(w * rows * 2 + j, nodes, stride=16), :] = zero
                gs[pl.ds(w * rows * 2 + j + 8, nodes, stride=16), :] = zero
    x = [xn[w * rows : (w + 1) * rows, :] for w in range(windows)]
    live = x[BEFORE // LANES][:, BEFORE % LANES : BEFORE % LANES + 1] < LIMIT
    x = [jnp.where(v < LIMIT, v, 0.0).astype(BF16) for v in x] + [jnp.zeros((rows, LANES), BF16)]
    x = jnp.concatenate([jnp.concatenate(x[w : w + 2], axis=1) for w in range(windows)], axis=0)
    sums = [[None] * nodes for _ in range(windows)]
    for a0 in range(0, FN, 2):
        count = min(2, FN - a0)
        y = contract_lanes(x, tt1[a0 * LANES : (a0 + count) * LANES, :])
        for a in range(a0, a0 + count):
            for w in range(windows):
                for n in range(nodes):
                    m = n + a - FN // 2
                    if 0 <= m < nodes:
                        row = w * rows + m * 8
                        v = y[row : row + 8, (a - a0) * LANES : (a - a0 + 1) * LANES]
                        sums[w][n] = v if sums[w][n] is None else sums[w][n] + v
    position = t * samples - LEAD + lax.broadcasted_iota(jnp.int32, (1, span), 1)
    valid = (position >= 0) & (position < total)
    for w in range(windows):
        inside = valid[:, w * LANES : (w + 1) * LANES]
        for n in range(nodes):
            f = jnp.where(live[n * 8 : n * 8 + 8, :] & inside, sums[w][n], 0.0)
            gs[(w * nodes + n) * 16 : (w * nodes + n) * 16 + 8, :] = f.astype(BF16).astype(F32)
    wh[...] = wx[...]
    wh[:, :, 0:depth] = hidden[...]
    delays = small[1:2, :]
    lane = lax.broadcasted_iota(jnp.int32, (1, LANES), 1)
    own = []
    for j in range(6):
        f = jnp.concatenate([gs[pl.ds(w * rows * 2 + j, nodes, stride=16), :] for w in range(windows)], axis=1)
        if 2 <= j < 4:
            own.append(f)
        shot = jnp.clip(2 * chip - 2 + j, 0, shots - 1)
        delay = jnp.sum(jnp.where(lane == shot, delays, 0.0)).astype(jnp.int32)
        r = jnp.where(valid, pltpu.roll(f, span - delay, 1), 0.0)
        for w in range(windows):
            gs[pl.ds(w * rows * 2 + j + 8, nodes, stride=16), :] = r[:, w * LANES : (w + 1) * LANES]
    row = lax.broadcasted_iota(jnp.int32, (16, span), 0)
    extra = jnp.where(row < 3, 1.0, jnp.where((row == 3) & ~valid, 1.0, 0.0)).astype(BF16)
    acts = []
    for n in range(nodes):
        tiles = [gs[(w * nodes + n) * 16 : (w * nodes + n + 1) * 16, :].astype(BF16) for w in range(windows)]
        columns = jnp.concatenate(taps_of(tiles, 1) + [extra], axis=0)
        act = jnp.dot(w0[...], columns, preferred_element_type=F32)
        acts.append(jnp.maximum(act.astype(BF16), 0.0))
    for layer in range(HID):
        for n in range(nodes):
            tiles = [acts[n][:, w * LANES : (w + 1) * LANES] for w in range(windows)]
            columns = jnp.concatenate(taps_of(tiles, 2 ** (layer + 1)) + [extra], axis=0)
            act = jnp.dot(wh[layer][:, 0 : depth + 16], columns, preferred_element_type=F32)
            acts[n] = jnp.maximum(act.astype(BF16), 0.0)
    pred = jnp.dot(ow[...], jnp.concatenate(acts, axis=0), preferred_element_type=F32) + small[0:1, 0:1]
    pred = pred.astype(BF16).astype(F32)
    own = jnp.where(odd, own[1], own[0])
    pred = jnp.where(alive & valid, pred, 0.0)
    interference[...] = pltpu.roll(pred, span - LEAD, 1)[:, 0:samples].astype(BF16)
    difference = (own - pred).astype(BF16)
    zp[0:8, :] = jnp.zeros((8, zp.shape[1]), F32)
    zp[nodes + 8 : nodes + 16, :] = jnp.zeros((8, zp.shape[1]), F32)
    for w in range(samples // LANES):
        zp[8 : 8 + nodes, :] = contract_lanes(difference[:, w * LANES : w * LANES + window], tt2[...])
        acc = None
        for a in range(FN):
            v = zp[8 + a - FN // 2 : 8 + a - FN // 2 + nodes, a * LANES : (a + 1) * LANES]
            acc = v if acc is None else acc + v
        cleaned[:, w * LANES : (w + 1) * LANES] = jnp.where(alive, acc, 0.0).astype(BF16)


def local(
    records,
    live,
    dither,
    designature,
    first_weights,
    first_bias,
    hidden_weights,
    hidden_bias,
    out_weights,
    out_bias,
    shaping,
    shots,
    parts,
):
    _, nodes, samples = records.shape
    channels = first_weights.shape[0]
    total = samples * parts
    window = 2 * LANES
    windows = samples // LANES + 1
    span = windows * LANES
    times, partner, pairs = exchanges(shots, parts)

    def send(x, pairs):
        return lax.ppermute(x, AXES, pairs)


    vmem = pl.BlockSpec(memory_space=pltpu.VMEM)
    tt1, tt2, w0, wx, ow, small = pl.pallas_call(
        prepare,
        out_shape=(
            jax.ShapeDtypeStruct((FN * LANES, window), BF16),
            jax.ShapeDtypeStruct((FN * LANES, window), BF16),
            jax.ShapeDtypeStruct((channels, 64), BF16),
            jax.ShapeDtypeStruct((HID, channels, window), BF16),
            jax.ShapeDtypeStruct((nodes, nodes * channels), BF16),
            jax.ShapeDtypeStruct((8, LANES), F32),
        ),
        in_specs=[vmem] * 8,
        out_specs=(vmem,) * 6,
        scratch_shapes=[pltpu.VMEM((16, window), F32)],
        compiler_params=pltpu.CompilerParams(vmem_limit_bytes=VMEM_LIMIT),
        cost_estimate=pl.CostEstimate(flops=10**8, bytes_accessed=10**7, transcendentals=0),
        name="prepare",
    )(
        dither[None],
        designature,
        shaping,
        first_weights.T,
        first_bias[None],
        hidden_bias,
        out_weights[None],
        out_bias[None],
    )

    keep = live[:, :, None] > 0
    dead = jnp.asarray(DEAD, BF16)
    around = [send(records, times[k]) for k in range(3)]
    mine = lax.optimization_barrier(jnp.where(keep, records, dead))
    x = pl.pallas_call(
        functools.partial(frame_of, parts),
        out_shape=jax.ShapeDtypeStruct((1, nodes, span), BF16),
        in_specs=[vmem] * 4,
        out_specs=vmem,
        compiler_params=pltpu.CompilerParams(vmem_limit_bytes=VMEM_LIMIT),
        name="frame",
    )(*around, mine)
    pair = jnp.concatenate([x, send(x, partner)], axis=0)
    near = [send(pair, pairs[k]) for k in range(3)]

    interference, cleaned = pl.pallas_call(
        functools.partial(deblend, total, shots),
        out_shape=(jax.ShapeDtypeStruct((nodes, samples), BF16),) * 2,
        in_specs=[vmem] * 11,
        out_specs=(vmem,) * 2,
        scratch_shapes=[
            pltpu.VMEM((windows * nodes * 8, LANES), F32),
            pltpu.VMEM((windows * nodes * 16, LANES), F32),
            pltpu.VMEM((nodes + 16, FN * LANES), F32),
            pltpu.VMEM((HID, channels, window), BF16),
        ],
        compiler_params=pltpu.CompilerParams(vmem_limit_bytes=VMEM_LIMIT),
        cost_estimate=pl.CostEstimate(flops=4 * 10**8, bytes_accessed=10**6, transcendentals=0),
        name="deblend",
    )(pair, *near, tt1, tt2, w0, hidden_weights, wx, ow, small)
    return interference[None], cleaned[None]


def solution(mesh):
    shots, parts = mesh.shape["shot"], mesh.shape["tm"]
    in_specs = (P("shot", None, "tm"), P("shot", None), P(), P(), P(), P(), P(), P(), P(), P(), P())
    out_specs = (P("shot", None, "tm"), P("shot", None, "tm"))

    def body(*args):
        return local(*args, shots=shots, parts=parts)

    return jax.shard_map(body, mesh=mesh, in_specs=in_specs, out_specs=out_specs, check_vma=False)
```
